1024 devices in a mesh: section: 4 (over y), dp: 8 (over x, core), expert: 32 (over z).
Axes of the slice: x: 4, y: 4, z: 32, core: 2. Of those that a mesh axis runs over, the one named last changes fastest.
Arguments:
- tokens_in: bfloat16 [4, 32768, 3072], P('section', ('dp', 'expert')), may hold values from -6 to 6
- upstream: bfloat16 [4, 32768, 3072], P('section', ('dp', 'expert')), may hold values from -6 to 6
- routes: int32 [4, 32768, 2], P('section', ('dp', 'expert')), may hold values from 0 to 31, as said below
- combine: bfloat16 [4, 32768, 2], P('section', ('dp', 'expert')), may hold values from 0.099609375 to 0.8984375
- gate_proj: bfloat16 [4, 32, 3072, 128], P('section', 'expert'), may hold values from -0.109375 to 0.109375
- up_proj: bfloat16 [4, 32, 3072, 128], P('section', 'expert'), may hold values from -0.109375 to 0.109375
- down_proj: bfloat16 [4, 32, 3072, 128], P('section', 'expert'), may hold values from -0.5 to 0.5
Outputs:
- prev_grad: bfloat16 [4, 32768, 3072], P('section', ('dp', 'expert'))
- weight_grad: float32 [4, 32, 3072, 384], P('section', 'expert', 'dp')
- combine_grad: bfloat16 [4, 32768, 2], P('section', ('dp', 'expert'))
The draws below stay inside these ranges and needn't reach their ends.
Inputs may be any that keep to these rules, and one draw needn't show every extreme that they name: `routes`: each token names two different experts. Of the 128 tokens of one device, at most 9 name any one expert, and in every section and replica one expert is named by exactly 9 tokens of every device.
All inputs are finite; a program needn't handle non-finite values.
Results may differ from the reference program's by a relative error of at most 0.012.
Values may be sent and summed in bfloat16 or wider, within the bound.
No kernel may reach another device: no remote copies, remote signals or barrier semaphores. Data moves between devices by JAX's collectives and lax.ppermute only.
A program may use at most 64 MiB of HBM per device.

```python
from functools import partial
import jax
import jax.numpy as jnp
from jax import lax

D = 3072
FF_DEV = 128
TOK_DEV = 128
SECTIONS = 4
REPLICAS = 8
EXPERTS = 32
CAP = 9
TOKENS = 32768


def draw_routes(key, part):
    blocks = SECTIONS * REPLICAS * EXPERTS
    entries = EXPERTS * CAP
    dropped_count = entries - 2 * TOK_DEV
    busiest_all = jax.random.randint(jax.random.fold_in(key, 11), (SECTIONS * REPLICAS,), 0, EXPERTS, dtype=jnp.int32)

    def one_block(block_index):
        block_key = jax.random.fold_in(key, block_index + 101)
        busiest = busiest_all[block_index // EXPERTS]
        entry_ids = jnp.arange(entries, dtype=jnp.int32)
        owner_expert = entry_ids // CAP
        jitter = jax.random.randint(jax.random.fold_in(block_key, 1), (entries,), 0, 2 ** 18, dtype=jnp.int32)
        scores = jitter * entries + entry_ids + jnp.where(owner_expert == busiest, 2 ** 30, 0).astype(jnp.int32)
        ranked = jnp.argsort(scores)
        position = jnp.argsort(ranked).astype(jnp.int32)
        removed = (position < dropped_count).astype(jnp.int32)
        retained = jnp.argsort(removed * entries + entry_ids)[:2 * TOK_DEV].astype(jnp.int32)
        listed = retained // CAP
        shuffled = jax.random.permutation(jax.random.fold_in(block_key, 2), TOK_DEV).astype(jnp.int32)
        first_pick = listed[shuffled]
        second_pick = listed[shuffled + TOK_DEV]
        return jnp.stack([first_pick, second_pick], axis=1)
    chosen = jax.vmap(one_block)(jnp.arange(blocks, dtype=jnp.int32))
    return chosen.reshape(SECTIONS, TOKENS, 2).astype(jnp.int32)


def block_levels(rng, extent, cuts, least, high):
    gain = 1.0
    for dim, blocks in cuts:
        draws = jax.random.uniform(jax.random.fold_in(jax.random.fold_in(rng, 6), dim), (blocks,), jnp.float32, least / len(cuts), high / len(cuts))
        gain = gain * jnp.repeat(jnp.exp(draws), extent[dim] // blocks).reshape((-1,) + (1,) * (len(extent) - 1 - dim))
    return gain


def centred(rng, extent, width, reach, split=(), kind=jnp.bfloat16):
    result = jax.random.normal(rng, extent, jnp.float32) * width
    if len(split) > 0:
        result = block_levels(rng, extent, split, -0.22, 0.18) * result
    return jnp.clip(result, min=-reach, max=reach).astype(kind)


def setup_inputs(seed: int = 0) -> dict:
    streams_of = jax.random.split(jax.random.key(seed), 8)
    return {
        "tokens_in": centred(streams_of[0], (SECTIONS, TOKENS, D), 1.0, 6.0, ((0, 4), (1, 256))),
        "upstream": centred(streams_of[1], (SECTIONS, TOKENS, D), 1.0, 6.0, ((0, 4), (1, 256))),
        "routes": draw_routes(jax.random.fold_in(streams_of[7], 71), 0),
        "combine": jnp.clip(0.099609375 + 0.7988281 * jax.random.uniform(streams_of[3], (SECTIONS, TOKENS, 2), jnp.float32) ** block_levels(streams_of[3], (SECTIONS, TOKENS, 2), ((0, 4), (1, 256)), -0.2, 0.2), 0.099609375, 0.8984375).astype(jnp.bfloat16),
        "gate_proj": centred(streams_of[4], (SECTIONS, EXPERTS, D, FF_DEV), D ** -0.5, 0.109375, ((0, 4), (1, 32))),
        "up_proj": centred(streams_of[5], (SECTIONS, EXPERTS, D, FF_DEV), D ** -0.5, 0.109375, ((0, 4), (1, 32))),
        "down_proj": centred(streams_of[6], (SECTIONS, EXPERTS, D, FF_DEV), FF_DEV ** -0.5, 0.5, ((0, 4), (1, 32))),
    }


def place_slots(chosen, expert_count, capacity):
    assigned = chosen.shape[0]
    onehot = (chosen[:, None] == jnp.arange(expert_count, dtype=jnp.int32)[None, :]).astype(jnp.int32)
    before = jnp.cumsum(onehot, axis=0).astype(jnp.int32) - onehot
    within = jnp.sum(before * onehot, axis=1).astype(jnp.int32)
    target = (chosen.astype(jnp.int32) * capacity + within).astype(jnp.int32)
    filler = jnp.full((expert_count * capacity,), assigned, jnp.int32)
    filler = filler.at[target].set(jnp.arange(assigned, dtype=jnp.int32))
    return target, filler


def fill_rows(token_rows, filler):
    padded = jnp.concatenate([token_rows, jnp.zeros((1, token_rows.shape[1]), token_rows.dtype)], axis=0)
    return jnp.take(padded, filler // 2, axis=0)


def fill_weights(weight_flat, filler):
    padded = jnp.concatenate([weight_flat, jnp.zeros((1,), weight_flat.dtype)])
    return jnp.take(padded, filler, axis=0)


def expert_pass(slot_rows, slot_grads, slot_weights, gate_w, up_w, down_w):
    rows_wide = slot_rows.astype(jnp.float32)
    gate = jnp.einsum("erd,edf->erf", rows_wide, gate_w.astype(jnp.float32))
    upper = jnp.einsum("erd,edf->erf", rows_wide, up_w.astype(jnp.float32))
    active = jax.nn.silu(gate)
    hidden = (active * upper).astype(jnp.bfloat16)
    output = jnp.einsum("erf,edf->erd", hidden.astype(jnp.float32), down_w.astype(jnp.float32))
    grads_wide = slot_grads.astype(jnp.float32)
    gate_slot = jnp.sum(output * grads_wide, axis=2).astype(jnp.bfloat16)
    d_output = (slot_weights.astype(jnp.float32)[:, :, None] * grads_wide).astype(jnp.bfloat16)
    d_hidden = jnp.einsum("erd,edf->erf", d_output.astype(jnp.float32), down_w.astype(jnp.float32))
    sigma = jax.nn.sigmoid(gate)
    d_gate = (d_hidden * upper * (sigma * (1.0 + gate * (1.0 - sigma)))).astype(jnp.bfloat16)
    d_up = (d_hidden * active).astype(jnp.bfloat16)
    slot_grad = jnp.einsum("erf,edf->erd", d_gate.astype(jnp.float32), gate_w.astype(jnp.float32))
    slot_grad = slot_grad + jnp.einsum("erf,edf->erd", d_up.astype(jnp.float32), up_w.astype(jnp.float32))
    slot_grad = slot_grad.astype(jnp.bfloat16)
    terms = jnp.concatenate([
        jnp.einsum("erd,erf->edf", rows_wide, d_gate.astype(jnp.float32)),
        jnp.einsum("erd,erf->edf", rows_wide, d_up.astype(jnp.float32)),
        jnp.einsum("erd,erf->edf", d_output.astype(jnp.float32), hidden.astype(jnp.float32)),
    ], axis=2)
    return gate_slot, slot_grad, terms


def to_experts(sent):
    shaped = sent.reshape((EXPERTS, EXPERTS, CAP) + sent.shape[2:])
    moved = jnp.swapaxes(shaped, 0, 1)
    return moved.reshape((EXPERTS, EXPERTS * CAP) + sent.shape[2:])


def per_replica(running, replica_parts, gate_w, up_w, down_w):
    rows_r, grads_r, routes_r, combine_r = replica_parts
    chosen = routes_r.reshape(EXPERTS, 2 * TOK_DEV)
    target, filler = jax.vmap(partial(place_slots, expert_count=EXPERTS, capacity=CAP))(chosen)
    sent_rows = to_experts(jax.vmap(fill_rows)(rows_r, filler))
    sent_grads = to_experts(jax.vmap(fill_rows)(grads_r, filler))
    sent_weights = to_experts(jax.vmap(fill_weights)(combine_r.reshape(EXPERTS, 2 * TOK_DEV), filler))
    gate_slot, slot_grad, terms = expert_pass(sent_rows, sent_grads, sent_weights, gate_w, up_w, down_w)
    rounded = lax.optimization_barrier(terms.astype(jnp.bfloat16))
    running = running + rounded.astype(jnp.float32)
    back_grad = to_experts(slot_grad)
    back_gate = to_experts(gate_slot)
    picked = jax.vmap(partial(jnp.take, axis=0))(back_grad, target)
    picked = picked.reshape(EXPERTS, TOK_DEV, 2, D).astype(jnp.float32)
    token_grad = jnp.sum(picked, axis=2).astype(jnp.bfloat16).reshape(EXPERTS * TOK_DEV, D)
    gate_pick = jax.vmap(partial(jnp.take, axis=0))(back_gate, target)
    return running, (token_grad, gate_pick.reshape(EXPERTS * TOK_DEV, 2))


def per_section(section_parts):
    rows_s, grads_s, routes_s, combine_s, gate_w, up_w, down_w = section_parts
    replica_parts = (
        rows_s.reshape(REPLICAS, EXPERTS, TOK_DEV, D),
        grads_s.reshape(REPLICAS, EXPERTS, TOK_DEV, D),
        routes_s.reshape(REPLICAS, EXPERTS, TOK_DEV, 2),
        combine_s.reshape(REPLICAS, EXPERTS, TOK_DEV, 2),
    )
    start = jnp.zeros((EXPERTS, D, 3 * FF_DEV), jnp.float32)
    step_fn = partial(per_replica, gate_w=gate_w, up_w=up_w, down_w=down_w)
    running, (token_grad, gate_pick) = lax.scan(step_fn, start, replica_parts)
    return token_grad.reshape(TOKENS, D), running * (1.0 / REPLICAS), gate_pick.reshape(TOKENS, 2)


def reference(tokens_in, upstream, routes, combine, gate_proj, up_proj, down_proj):
    token_grad, weight_grad, combine_grad = lax.map(per_section, (tokens_in, upstream, routes, combine, gate_proj, up_proj, down_proj))
    prev_grad = jnp.roll(token_grad, -1, axis=0)
    return prev_grad, weight_grad, combine_grad
```

```python
import jax
import jax.numpy as jnp
from jax import lax
from jax.experimental import pallas as pl
from jax.experimental.pallas import tpu as pltpu
from jax.sharding import PartitionSpec as P


INTERPRET = False
F32 = jnp.float32
BF16 = jnp.bfloat16
SUB = 8
EXTRA = 128


def shifted(value, axis, steps):
    count = lax.axis_size(axis)
    return lax.ppermute(value, axis, [(s, (s + steps) % count) for s in range(count)])


def offsets_of(reach):
    return list(range(-reach, reach + 1))


def blocks_of(d, reach):
    return (d + reach,) if abs(d) == reach else (d + reach, d + 3 * reach)


def selectors(routes_ref, here, experts):
    reach = experts // 4
    tokens = routes_ref.shape[1]
    ids = lax.broadcasted_iota(jnp.int32, (experts, tokens), 0)
    picks = [routes_ref[k : k + 1, :] for k in range(2)]
    named = [jnp.where(ids == p, 1.0, 0.0) for p in picks]
    earlier = lax.broadcasted_iota(jnp.int32, (tokens, tokens), 0) < lax.broadcasted_iota(
        jnp.int32, (tokens, tokens), 1
    )
    before = jnp.dot(
        (named[0] + named[1]).astype(BF16),
        jnp.where(earlier, 1.0, 0.0).astype(BF16),
        preferred_element_type=F32,
    )
    row = lax.broadcasted_iota(jnp.int32, (experts * SUB, tokens), 0)
    main, ninth = [], []
    for p, hit in zip(picks, named):
        slot = jnp.sum(before * hit, axis=0, keepdims=True).astype(jnp.int32)
        block = p - here + reach
        block = jnp.where(block < 0, block + experts, block)
        block = jnp.where(block >= experts, block - experts, block)
        main.append(jnp.where(row == jnp.where(slot < SUB, block * SUB + slot, -1), 1.0, 0.0))
        ninth.append(jnp.where((row >> 3) == jnp.where(slot == SUB, block, -1), 1.0, 0.0))
    return main, ninth, row & (SUB - 1)


def pack_kernel(here_ref, routes_ref, combine_ref, rows_ref, grads_ref, *outs, experts):
    reach = experts // 4
    width = rows_ref.shape[1]
    fold = width // SUB
    main, ninth, sub = selectors(routes_ref, here_ref[0], experts)
    weights = [combine_ref[k : k + 1, :].astype(F32) for k in range(2)]
    for kind, ref in enumerate((rows_ref, grads_ref)):
        if kind == 0:
            pick = main[0] + main[1]
            pick9 = ninth[0] + ninth[1]
        else:
            pick = main[0] * weights[0] + main[1] * weights[1]
            pick9 = ninth[0] * weights[0] + ninth[1] * weights[1]
        body = jnp.dot(pick.astype(BF16), ref[...], preferred_element_type=F32)
        tail = jnp.zeros((experts * SUB, fold), F32)
        for s in range(SUB):
            tail = tail + jnp.dot(
                jnp.where(sub == s, pick9, 0.0).astype(BF16),
                ref[:, s * fold : (s + 1) * fold],
                preferred_element_type=F32,
            )
        for d, out in zip(offsets_of(reach), outs):
            for i, b in enumerate(blocks_of(d, reach)):
                at = slice(b * SUB, (b + 1) * SUB)
                out[2 * i + kind, :, 0:width] = body[at, :].astype(BF16)
                out[2 * i + kind, :, width : width + fold] = tail[at, :].astype(BF16)


def pack(here, routes_t, combine_t, rows, grads, experts):
    reach = experts // 4
    width = rows.shape[1]
    vmem = pl.BlockSpec(memory_space=pltpu.VMEM)
    shapes = [
        jax.ShapeDtypeStruct((2 * len(blocks_of(d, reach)), SUB, width + width // SUB), BF16)
        for d in offsets_of(reach)
    ]
    return pl.pallas_call(
        lambda *refs: pack_kernel(*refs, experts=experts),
        out_shape=shapes,
        in_specs=[pl.BlockSpec(memory_space=pltpu.SMEM)] + [vmem] * 4,
        out_specs=[vmem] * len(shapes),
        name="pack",
        interpret=INTERPRET,
    )(here, routes_t, combine_t, rows, grads)


def gather_blocks(ref_of, count, scratch, folded, width, picks):
    fold = width // SUB
    for b in range(count):
        block = ref_of(b)
        scratch[b * SUB : (b + 1) * SUB, :] = block[:, 0:width]
        folded[b * SUB : (b + 1) * SUB, :] = block[:, width : width + fold]
    whole = folded[0 : count * SUB, :]
    for s in range(SUB):
        nine = jnp.dot(picks[s], whole, preferred_element_type=F32).astype(BF16)
        scratch[count * SUB : count * SUB + nine.shape[0], s * fold : (s + 1) * fold] = nine


def expert_kernel(*refs, experts):
    reach = experts // 4
    offsets = offsets_of(reach)
    arrived = refs[: len(offsets)]
    own_w = refs[len(offsets) : len(offsets) + 3]
    far_w = refs[len(offsets) + 3]
    at = len(offsets) + 4
    returned = refs[at : at + len(offsets)]
    terms = refs[at + len(offsets) : at + len(offsets) + 2]
    x_ref, g_ref, folded = refs[at + len(offsets) + 2 :]
    width = own_w[0].shape[0]
    ff = own_w[0].shape[1]
    fold = width // SUB
    by_hidden = (((1,), (1,)), ((), ()))
    by_rows = (((0,), (0,)), ((), ()))
    for half in range(2):
        reached = reach if half == 0 else reach - 1
        here = [(d, arrived[d + reach]) for d in range(-reached, reached + 1)]
        count = len(here)
        padded = -(-count // SUB) * SUB
        rows = count * SUB + padded
        r0 = lax.broadcasted_iota(jnp.int32, (padded, count * SUB), 0)
        r1 = lax.broadcasted_iota(jnp.int32, (padded, count * SUB), 1)
        picks = [jnp.where(r1 == r0 * SUB + s, 1.0, 0.0).astype(BF16) for s in range(SUB)]
        gather_blocks(lambda b: here[b][1].at[2 * half], count, x_ref, folded, width, picks)
        gather_blocks(lambda b: here[b][1].at[2 * half + 1], count, g_ref, folded, width, picks)
        if half == 0:
            gate_w, up_w, down_w = [w[...] for w in own_w]
        else:
            gate_w, up_w, down_w = [far_w[:, i].reshape(width, ff) for i in range(3)]
        x = x_ref[0:rows, :]
        g = g_ref[0:rows, :]
        gate = jnp.dot(x, gate_w, preferred_element_type=F32)
        upper = jnp.dot(x, up_w, preferred_element_type=F32)
        d_hidden = jnp.dot(g, down_w, preferred_element_type=F32)
        sigma = jax.nn.sigmoid(gate)
        active = gate * sigma
        hidden = (active * upper).astype(BF16)
        weighed = jnp.sum(hidden.astype(F32) * d_hidden, axis=1, keepdims=True)
        d_gate = (d_hidden * upper * (sigma * (1.0 + gate * (1.0 - sigma)))).astype(BF16)
        d_up = (d_hidden * active).astype(BF16)
        slot_grad = lax.dot_general(d_gate, gate_w, by_hidden, preferred_element_type=F32)
        slot_grad = slot_grad + lax.dot_general(d_up, up_w, by_hidden, preferred_element_type=F32)
        nine = slot_grad[count * SUB :, :].astype(BF16)
        q0 = lax.broadcasted_iota(jnp.int32, (count * SUB, padded), 0)
        q1 = lax.broadcasted_iota(jnp.int32, (count * SUB, padded), 1)
        tail = jnp.zeros((count * SUB, fold), F32)
        spread = []
        for s in range(SUB):
            put = jnp.where(q0 == q1 * SUB + s, 1.0, 0.0).astype(BF16)
            spread.append(put)
            tail = tail + jnp.dot(put, nine[:, s * fold : (s + 1) * fold], preferred_element_type=F32)
        nine_sum = jnp.broadcast_to(weighed[count * SUB :, :], (padded, EXTRA)).astype(BF16)
        nine_sum = jnp.dot(spread[0], nine_sum, preferred_element_type=F32)
        lane = lax.broadcasted_iota(jnp.int32, (count * SUB, EXTRA), 1)
        extra = jnp.where(lane == 0, weighed[0 : count * SUB, :], jnp.where(lane == 1, nine_sum, 0.0))
        for b, (d, _) in enumerate(here):
            out = returned[d + reach]
            span = slice(b * SUB, (b + 1) * SUB)
            out[half, :, 0:width] = slot_grad[span, :].astype(BF16)
            out[half, :, width : width + fold] = tail[span, :].astype(BF16)
            out[half, :, width + fold : width + fold + EXTRA] = extra[span, :].astype(BF16)
        term = terms[half]
        term[:, 0:ff] = lax.dot_general(x, d_gate, by_rows, preferred_element_type=F32).astype(BF16)
        term[:, ff : 2 * ff] = lax.dot_general(x, d_up, by_rows, preferred_element_type=F32).astype(
            BF16
        )
        term[:, 2 * ff : 3 * ff] = lax.dot_general(
            g, hidden, by_rows, preferred_element_type=F32
        ).astype(BF16)


def run_experts(arrived, own_w, far_w, experts):
    reach = experts // 4
    width, ff = own_w[0].shape
    fold = width // SUB
    vmem = pl.BlockSpec(memory_space=pltpu.VMEM)
    shapes = [
        jax.ShapeDtypeStruct((len(blocks_of(d, reach)), SUB, width + fold + EXTRA), BF16)
        for d in offsets_of(reach)
    ] + [jax.ShapeDtypeStruct((width, 3 * ff), BF16)] * 2
    count = 2 * reach + 1
    rows = count * SUB + -(-count // SUB) * SUB
    outs = pl.pallas_call(
        lambda *refs: expert_kernel(*refs, experts=experts),
        out_shape=shapes,
        in_specs=[vmem] * (len(arrived) + 4),
        out_specs=[vmem] * len(shapes),
        scratch_shapes=[
            pltpu.VMEM((rows, width), BF16),
            pltpu.VMEM((rows, width), BF16),
            pltpu.VMEM((count * SUB, fold), BF16),
        ],
        name="experts",
        interpret=INTERPRET,
    )(*arrived, *own_w, far_w)
    return outs[:-2], outs[-2], outs[-1]


def unpack_kernel(here_ref, routes_ref, combine_ref, *refs, experts):
    reach = experts // 4
    offsets = offsets_of(reach)
    arrived = refs[: len(offsets)]
    grad_out, combine_out, body, tail, extra = refs[len(offsets) :]
    width = body.shape[1]
    fold = tail.shape[1]
    for d, ref in zip(offsets, arrived):
        for i, b in enumerate(blocks_of(d, reach)):
            span = slice(b * SUB, (b + 1) * SUB)
            body[span, :] = ref[i, :, 0:width]
            tail[span, :] = ref[i, :, width : width + fold]
            extra[span, :] = ref[i, :, width + fold : width + fold + EXTRA].astype(F32)
    main, ninth, sub = selectors(routes_ref, here_ref[0], experts)
    pick = (main[0] + main[1]).T.astype(BF16)
    nine = ninth[0] + ninth[1]
    for s in range(SUB):
        cols = slice(s * fold, (s + 1) * fold)
        total = jnp.dot(pick, body[:, cols], preferred_element_type=F32)
        total = total + jnp.dot(
            jnp.where(sub == s, nine, 0.0).T.astype(BF16), tail[...], preferred_element_type=F32
        )
        grad_out[:, cols] = total.astype(BF16)
    for k in range(2):
        value = main[k] * extra[:, 0:1] + jnp.where(sub == 0, ninth[k], 0.0) * extra[:, 1:2]
        value = jnp.sum(value, axis=0, keepdims=True)
        combine_out[k : k + 1, :] = value / combine_ref[k : k + 1, :].astype(F32)


def unpack(here, routes_t, combine_t, arrived, width, experts):
    tokens = routes_t.shape[1]
    vmem = pl.BlockSpec(memory_space=pltpu.VMEM)
    return pl.pallas_call(
        lambda *refs: unpack_kernel(*refs, experts=experts),
        out_shape=[
            jax.ShapeDtypeStruct((tokens, width), BF16),
            jax.ShapeDtypeStruct((2, tokens), F32),
        ],
        in_specs=[pl.BlockSpec(memory_space=pltpu.SMEM)] + [vmem] * (2 + len(arrived)),
        out_specs=[vmem] * 2,
        scratch_shapes=[
            pltpu.VMEM((experts * SUB, width), BF16),
            pltpu.VMEM((experts * SUB, width // SUB), BF16),
            pltpu.VMEM((experts * SUB, EXTRA), F32),
        ],
        name="unpack",
        interpret=INTERPRET,
    )(here, routes_t, combine_t, *arrived)


def spread_over(x, axis):
    copies = jnp.broadcast_to(x[None], (lax.axis_size(axis),) + x.shape)
    return lax.all_to_all(copies, axis, split_axis=0, concat_axis=0, tiled=True)


def summed_on_arrival(term, axis):
    count = lax.axis_size(axis)
    pieces = term.reshape(count, term.shape[0] // count, term.shape[1])
    arrived = lax.all_to_all(pieces, axis, split_axis=0, concat_axis=0, tiled=True)
    return arrived.astype(F32).sum(axis=0)


def per_device(tokens_in, upstream, routes, combine, gate_proj, up_proj, down_proj):
    experts = lax.axis_size("expert")
    replicas = lax.axis_size("dp")
    reach = experts // 4
    width = tokens_in.shape[2]
    assert 9 * tokens_in.shape[1] == 4 * experts * (SUB + 1)
    here = lax.axis_index("expert").astype(jnp.int32).reshape(1)
    routes_t = routes[0].T
    combine_t = combine[0].T
    own_w = [w[0, 0] for w in (gate_proj, up_proj, down_proj)]
    part = width // replicas
    start = lax.axis_index("dp") * part
    offsets = offsets_of(reach)
    piece = jnp.stack([lax.dynamic_slice_in_dim(w, start, part, 0) for w in own_w])
    piece = shifted(piece, "expert", 2 * reach)
    far_w = spread_over(piece, "dp")
    packed = pack(here, routes_t, combine_t, tokens_in[0], upstream[0], experts)
    arrived = list(packed)
    for i, d in enumerate(offsets):
        if d:
            arrived[i] = shifted(packed[i], "expert", d)
    done, own_term, far_term = run_experts(arrived, own_w, far_w, experts)
    back = list(done)
    for i, d in enumerate(offsets):
        if d:
            back[i] = shifted(done[i], "expert", -d)
    far_sum = summed_on_arrival(far_term, "dp").astype(BF16)
    far_sum = shifted(far_sum, "expert", 2 * reach)
    own_sum = summed_on_arrival(own_term, "dp")
    weight_grad = (own_sum + far_sum.astype(F32)) * (1.0 / replicas)
    token_grad, combine_grad = unpack(here, routes_t, combine_t, back, width, experts)
    prev_grad = shifted(token_grad[None], "section", -1)
    return prev_grad, weight_grad[None, None], combine_grad.astype(BF16).T[None]


def solution(mesh):
    rows = P("section", ("dp", "expert"), None)
    weights = P("section", "expert", None, None)

    return jax.shard_map(
        per_device,
        mesh=mesh,
        in_specs=(rows, rows, rows, rows, weights, weights, weights),
        out_specs=(rows, P("section", "expert", "dp", None), rows),
        check_vma=False,
    )
```

```python
import jax
import jax.numpy as jnp
from jax import lax
from jax.experimental import pallas as pl
from jax.experimental.pallas import tpu as pltpu
from jax.sharding import PartitionSpec as P


INTERPRET = False
F32 = jnp.float32
BF16 = jnp.bfloat16
SUB = 8
EXTRA = 128


COPIES = 4


def shifted(value, axis, steps):
    count = lax.axis_size(axis)
    return lax.ppermute(value, axis, [(s, (s + steps) % count) for s in range(count)])


def sent_back(value, steps):
    sections, count = lax.axis_size("section"), lax.axis_size("expert")
    pairs = [
        (s * count + e, (s - 1) % sections * count + (e + steps) % count)
        for s in range(sections)
        for e in range(count)
    ]
    return lax.ppermute(value, ("section", "expert"), pairs)


def offsets_of(reach):
    return list(range(-reach, reach + 1))


def hosts_of(d, reach):
    return tuple(range(0, COPIES, 2)) if abs(d) == reach else tuple(range(COPIES))


def blocks_of(d, reach):
    return tuple((d + reach + 2 * reach * k) % (2 * reach * COPIES) for k in hosts_of(d, reach))


def selectors(routes_ref, here, experts):
    reach = experts // (2 * COPIES)
    tokens = routes_ref.shape[1]
    ids = lax.broadcasted_iota(jnp.int32, (experts, tokens), 0)
    picks = [routes_ref[k : k + 1, :] for k in range(2)]
    named = [jnp.where(ids == p, 1.0, 0.0) for p in picks]
    earlier = lax.broadcasted_iota(jnp.int32, (tokens, tokens), 0) < lax.broadcasted_iota(
        jnp.int32, (tokens, tokens), 1
    )
    before = jnp.dot(
        (named[0] + named[1]).astype(BF16),
        jnp.where(earlier, 1.0, 0.0).astype(BF16),
        preferred_element_type=F32,
    )
    row = lax.broadcasted_iota(jnp.int32, (experts * SUB, tokens), 0)
    main, ninth = [], []
    for p, hit in zip(picks, named):
        slot = jnp.sum(before * hit, axis=0, keepdims=True).astype(jnp.int32)
        block = p - here + reach
        block = jnp.where(block < 0, block + experts, block)
        block = jnp.where(block >= experts, block - experts, block)
        main.append(jnp.where(row == jnp.where(slot < SUB, block * SUB + slot, -1), 1.0, 0.0))
        ninth.append(jnp.where((row >> 3) == jnp.where(slot == SUB, block, -1), 1.0, 0.0))
    return main, ninth, row & (SUB - 1)


def pack_kernel(here_ref, routes_ref, combine_ref, rows_ref, grads_ref, *outs, experts):
    reach = experts // (2 * COPIES)
    width = rows_ref.shape[1]
    fold = width // SUB
    main, ninth, sub = selectors(routes_ref, here_ref[0], experts)
    weights = [combine_ref[k : k + 1, :].astype(F32) for k in range(2)]
    for kind, ref in enumerate((rows_ref, grads_ref)):
        if kind == 0:
            pick = main[0] + main[1]
            pick9 = ninth[0] + ninth[1]
        else:
            pick = main[0] * weights[0] + main[1] * weights[1]
            pick9 = ninth[0] * weights[0] + ninth[1] * weights[1]
        body = jnp.dot(pick.astype(BF16), ref[...], preferred_element_type=F32)
        tail = jnp.zeros((experts * SUB, fold), F32)
        for s in range(SUB):
            tail = tail + jnp.dot(
                jnp.where(sub == s, pick9, 0.0).astype(BF16),
                ref[:, s * fold : (s + 1) * fold],
                preferred_element_type=F32,
            )
        for d, out in zip(offsets_of(reach), outs):
            for i, b in enumerate(blocks_of(d, reach)):
                at = slice(b * SUB, (b + 1) * SUB)
                out[2 * i + kind, :, 0:width] = body[at, :].astype(BF16)
                out[2 * i + kind, :, width : width + fold] = tail[at, :].astype(BF16)


def pack(here, routes_t, combine_t, rows, grads, experts):
    reach = experts // (2 * COPIES)
    width = rows.shape[1]
    vmem = pl.BlockSpec(memory_space=pltpu.VMEM)
    shapes = [
        jax.ShapeDtypeStruct((2 * len(blocks_of(d, reach)), SUB, width + width // SUB), BF16)
        for d in offsets_of(reach)
    ]
    return pl.pallas_call(
        lambda *refs: pack_kernel(*refs, experts=experts),
        out_shape=shapes,
        in_specs=[pl.BlockSpec(memory_space=pltpu.SMEM)] + [vmem] * 4,
        out_specs=[vmem] * len(shapes),
        name="pack",
        interpret=INTERPRET,
    )(here, routes_t, combine_t, rows, grads)


def gather_blocks(blocks, scratch, folded, width, picks):
    fold = width // SUB
    count = len(blocks)
    for b, block in enumerate(blocks):
        scratch[b * SUB : (b + 1) * SUB, :] = block[:, 0:width]
        folded[b * SUB : (b + 1) * SUB, :] = block[:, width : width + fold]
    whole = folded[0 : count * SUB, :]
    for s in range(SUB):
        nine = jnp.dot(picks[s], whole, preferred_element_type=F32).astype(BF16)
        scratch[count * SUB : count * SUB + nine.shape[0], s * fold : (s + 1) * fold] = nine


def expert_kernel(*refs, experts):
    reach = experts // (2 * COPIES)
    offsets = offsets_of(reach)
    arrived = refs[: len(offsets)]
    own_w = refs[len(offsets) : len(offsets) + 3]
    side_w, far_w = refs[len(offsets) + 3 : len(offsets) + 5]
    at = len(offsets) + 5
    returned = refs[at : at + len(offsets)]
    own_t, side_t, far_t = refs[at + len(offsets) : at + len(offsets) + 3]
    x_ref, g_ref, folded = refs[at + len(offsets) + 3 :]
    width = own_w[0].shape[0]
    ff = own_w[0].shape[1]
    fold = width // SUB
    by_hidden = (((1,), (1,)), ((), ()))
    by_rows = (((0,), (0,)), ((), ()))
    for k in range(COPIES):
        here = [(d, hosts_of(d, reach).index(k)) for d in offsets if k in hosts_of(d, reach)]
        count = len(here)
        padded = -(-count // SUB) * SUB
        rows = count * SUB + padded
        r0 = lax.broadcasted_iota(jnp.int32, (padded, count * SUB), 0)
        r1 = lax.broadcasted_iota(jnp.int32, (padded, count * SUB), 1)
        picks = [jnp.where(r1 == r0 * SUB + s, 1.0, 0.0).astype(BF16) for s in range(SUB)]
        blocks = [arrived[d + reach].at[2 * i] for d, i in here]
        gather_blocks(blocks, x_ref, folded, width, picks)
        blocks = [arrived[d + reach].at[2 * i + 1] for d, i in here]
        gather_blocks(blocks, g_ref, folded, width, picks)
        if k == 0:
            gate_w, up_w, down_w = [w[...] for w in own_w]
        elif k == 2:
            gate_w, up_w, down_w = [far_w[:, i].reshape(width, ff) for i in range(3)]
        else:
            gate_w, up_w, down_w = [side_w[:, k // 2, i].reshape(width, ff) for i in range(3)]
        x = x_ref[0:rows, :]
        g = g_ref[0:rows, :]
        gate = jnp.dot(x, gate_w, preferred_element_type=F32)
        upper = jnp.dot(x, up_w, preferred_element_type=F32)
        d_hidden = jnp.dot(g, down_w, preferred_element_type=F32)
        sigma = jax.nn.sigmoid(gate)
        active = gate * sigma
        hidden = (active * upper).astype(BF16)
        weighed = jnp.sum(hidden.astype(F32) * d_hidden, axis=1, keepdims=True)
        d_gate = (d_hidden * upper * (sigma * (1.0 + gate * (1.0 - sigma)))).astype(BF16)
        d_up = (d_hidden * active).astype(BF16)
        slot_grad = lax.dot_general(d_gate, gate_w, by_hidden, preferred_element_type=F32)
        slot_grad = slot_grad + lax.dot_general(d_up, up_w, by_hidden, preferred_element_type=F32)
        nine = slot_grad[count * SUB :, :].astype(BF16)
        q0 = lax.broadcasted_iota(jnp.int32, (count * SUB, padded), 0)
        q1 = lax.broadcasted_iota(jnp.int32, (count * SUB, padded), 1)
        tail = jnp.zeros((count * SUB, fold), F32)
        spread = []
        for s in range(SUB):
            put = jnp.where(q0 == q1 * SUB + s, 1.0, 0.0).astype(BF16)
            spread.append(put)
            tail = tail + jnp.dot(put, nine[:, s * fold : (s + 1) * fold], preferred_element_type=F32)
        nine_sum = jnp.broadcast_to(weighed[count * SUB :, :], (padded, EXTRA)).astype(BF16)
        nine_sum = jnp.dot(spread[0], nine_sum, preferred_element_type=F32)
        lane = lax.broadcasted_iota(jnp.int32, (count * SUB, EXTRA), 1)
        extra = jnp.where(lane == 0, weighed[0 : count * SUB, :], jnp.where(lane == 1, nine_sum, 0.0))
        for b, (d, i) in enumerate(here):
            out = returned[d + reach]
            span = slice(b * SUB, (b + 1) * SUB)
            out[i, :, 0:width] = slot_grad[span, :].astype(BF16)
            out[i, :, width : width + fold] = tail[span, :].astype(BF16)
            out[i, :, width + fold : width + fold + EXTRA] = extra[span, :].astype(BF16)
        for i, (left, right) in enumerate(((x, d_gate), (x, d_up), (g, hidden))):
            cols = slice(i * ff, (i + 1) * ff)
            term = lax.dot_general(left, right, by_rows, preferred_element_type=F32).astype(BF16)
            if k == 0:
                own_t[:, :, cols] = term.reshape(own_t.shape[0], -1, ff)
            elif k == 2:
                far_t[:, :, cols] = term.reshape(far_t.shape[0], -1, ff)
            else:
                side_t[:, k // 2, :, cols] = term.reshape(side_t.shape[0], -1, ff)


def run_experts(arrived, own_w, side_w, far_w, experts):
    reach = experts // (2 * COPIES)
    width, ff = own_w[0].shape
    fold = width // SUB
    replicas = far_w.shape[0]
    vmem = pl.BlockSpec(memory_space=pltpu.VMEM)
    shapes = [
        jax.ShapeDtypeStruct((len(blocks_of(d, reach)), SUB, width + fold + EXTRA), BF16)
        for d in offsets_of(reach)
    ] + [
        jax.ShapeDtypeStruct((replicas,) + lead + (width // replicas, 3 * ff), BF16)
        for lead in ((), (2,), ())
    ]
    count = 2 * reach + 1
    rows = count * SUB + -(-count // SUB) * SUB
    outs = pl.pallas_call(
        lambda *refs: expert_kernel(*refs, experts=experts),
        out_shape=shapes,
        in_specs=[vmem] * (len(arrived) + 5),
        out_specs=[vmem] * len(shapes),
        scratch_shapes=[
            pltpu.VMEM((rows, width), BF16),
            pltpu.VMEM((rows, width), BF16),
            pltpu.VMEM((count * SUB, fold), BF16),
        ],
        name="experts",
        interpret=INTERPRET,
    )(*arrived, *own_w, side_w, far_w)
    return outs[:-3], outs[-3:]


def scalars_kernel(here_ref, routes_ref, combine_ref, *refs, experts):
    reach = experts // (2 * COPIES)
    offsets = offsets_of(reach)
    combine_out, extra = refs[len(offsets) :]
    for d, ref in zip(offsets, refs):
        for i, b in enumerate(blocks_of(d, reach)):
            extra[b * SUB : (b + 1) * SUB, :] = ref[i].astype(F32)
    main, ninth, sub = selectors(routes_ref, here_ref[0], experts)
    for k in range(2):
        value = main[k] * extra[:, 0:1] + jnp.where(sub == 0, ninth[k], 0.0) * extra[:, 1:2]
        value = jnp.sum(value, axis=0, keepdims=True)
        combine_out[k : k + 1, :] = value / combine_ref[k : k + 1, :]


def unpack_kernel(here_ref, routes_ref, *refs, experts):
    reach = experts // (2 * COPIES)
    offsets = offsets_of(reach)
    grad_out, body, tail = refs[len(offsets) :]
    width = body.shape[1]
    fold = tail.shape[1]
    for d, ref in zip(offsets, refs):
        for i, b in enumerate(blocks_of(d, reach)):
            span = slice(b * SUB, (b + 1) * SUB)
            body[span, :] = ref[i, :, 0:width]
            tail[span, :] = ref[i, :, width : width + fold]
    main, ninth, sub = selectors(routes_ref, here_ref[0], experts)
    pick = (main[0] + main[1]).T.astype(BF16)
    nine = ninth[0] + ninth[1]
    for s in range(SUB):
        cols = slice(s * fold, (s + 1) * fold)
        total = jnp.dot(pick, body[:, cols], preferred_element_type=F32)
        total = total + jnp.dot(
            jnp.where(sub == s, nine, 0.0).T.astype(BF16), tail[...], preferred_element_type=F32
        )
        grad_out[:, cols] = total.astype(BF16)


def unpack_scalars(here, routes_t, combine_t, arrived, width, experts):
    vmem = pl.BlockSpec(memory_space=pltpu.VMEM)
    at = (width + width // SUB) // EXTRA
    lanes = [pl.BlockSpec((a.shape[0], SUB, EXTRA), lambda i: (0, 0, at)) for a in arrived]
    return pl.pallas_call(
        lambda *refs: scalars_kernel(*refs, experts=experts),
        grid=(1,),
        out_shape=jax.ShapeDtypeStruct(routes_t.shape, F32),
        in_specs=[pl.BlockSpec(memory_space=pltpu.SMEM), vmem, vmem] + lanes,
        out_specs=vmem,
        scratch_shapes=[pltpu.VMEM((experts * SUB, EXTRA), F32)],
        name="scalars",
        interpret=INTERPRET,
    )(here, routes_t, combine_t, *arrived)


def unpack(here, routes_t, arrived, width, experts):
    vmem = pl.BlockSpec(memory_space=pltpu.VMEM)
    return pl.pallas_call(
        lambda *refs: unpack_kernel(*refs, experts=experts),
        out_shape=jax.ShapeDtypeStruct((routes_t.shape[1], width), BF16),
        in_specs=[pl.BlockSpec(memory_space=pltpu.SMEM)] + [vmem] * (1 + len(arrived)),
        out_specs=vmem,
        scratch_shapes=[
            pltpu.VMEM((experts * SUB, width), BF16),
            pltpu.VMEM((experts * SUB, width // SUB), BF16),
        ],
        name="unpack",
        interpret=INTERPRET,
    )(here, routes_t, *arrived)


def spread_over(x, axis):
    copies = jnp.broadcast_to(x[None], (lax.axis_size(axis),) + x.shape)
    return lax.all_to_all(copies, axis, split_axis=0, concat_axis=0, tiled=True)


def summed_on_arrival(pieces, axis):
    arrived = lax.all_to_all(pieces, axis, split_axis=0, concat_axis=0, tiled=True)
    return arrived.astype(F32).sum(axis=0)


def per_device(tokens_in, upstream, routes, combine, gate_proj, up_proj, down_proj):
    experts = lax.axis_size("expert")
    replicas = lax.axis_size("dp")
    reach = experts // (2 * COPIES)
    period = 2 * reach
    width = tokens_in.shape[2]
    tokens = tokens_in.shape[1]
    assert 9 * tokens == 4 * experts * (SUB + 1)
    here = lax.axis_index("expert").astype(jnp.int32).reshape(1)
    routes_t = routes[0].T
    combine_t = combine[0].T
    own_w = [w[0, 0] for w in (gate_proj, up_proj, down_proj)]
    part = width // replicas
    start = lax.axis_index("dp") * part
    offsets = offsets_of(reach)
    piece = jnp.stack([lax.dynamic_slice_in_dim(w, start, part, 0) for w in own_w])
    side1 = shifted(piece, "expert", -period)
    side3 = shifted(piece, "expert", period)
    low = shifted(side1[:, : part // 2], "expert", -period)
    high = shifted(side3[:, part // 2 :], "expert", period)
    side_w = spread_over(jnp.stack([side1, side3]), "dp")
    far_w = spread_over(jnp.concatenate([low, high], axis=1), "dp")
    packed = pack(here, routes_t, combine_t, tokens_in[0], upstream[0], experts)
    behind = shifted(jnp.concatenate([routes_t.astype(F32), combine_t.astype(F32)]), "section", -1)
    arrived = list(packed)
    for i, d in enumerate(offsets):
        if d:
            arrived[i] = shifted(packed[i], "expert", d)
    done, (own_t, side_t, far_t) = run_experts(arrived, own_w, side_w, far_w, experts)
    back = []
    for i, d in enumerate(offsets):
        back.append(sent_back(done[i], -d))
    far_sum = summed_on_arrival(far_t, "dp").astype(BF16)
    low = shifted(far_sum[: part // 2], "expert", period)
    high = shifted(far_sum[part // 2 :], "expert", -period)
    side_sum = summed_on_arrival(side_t, "dp")
    joined = jnp.concatenate([side_sum[0, : part // 2] + low.astype(F32), side_sum[0, part // 2 :]])
    side1 = shifted(joined.astype(BF16), "expert", period)
    joined = jnp.concatenate([side_sum[1, : part // 2], side_sum[1, part // 2 :] + high.astype(F32)])
    side3 = shifted(joined.astype(BF16), "expert", -period)
    own_sum = summed_on_arrival(own_t, "dp")
    weight_grad = (own_sum + side1.astype(F32) + side3.astype(F32)) * (1.0 / replicas)
    routes_b = behind[:2].astype(jnp.int32)
    combine_grad = unpack_scalars(here, routes_b, behind[2:], back, width, experts)
    combine_grad = shifted(combine_grad, "section", 1)
    prev_grad = unpack(here, routes_b, back, width, experts)
    return prev_grad[None], weight_grad[None, None], combine_grad.astype(BF16).T[None]


def solution(mesh):
    rows = P("section", ("dp", "expert"), None)
    weights = P("section", "expert", None, None)

    return jax.shard_map(
        per_device,
        mesh=mesh,
        in_specs=(rows, rows, rows, rows, weights, weights, weights),
        out_specs=(rows, P("section", "expert", "dp", None), rows),
        check_vma=False,
    )
```

```python
import jax
import jax.numpy as jnp
from jax import lax
from jax.experimental import pallas as pl
from jax.experimental.pallas import tpu as pltpu
from jax.sharding import PartitionSpec as P


INTERPRET = False
F32 = jnp.float32
BF16 = jnp.bfloat16
SUB = 8
EXTRA = 128


COPIES = 4
CORES = 2


def shifted(value, axis, steps):
    count = lax.axis_size(axis)
    return lax.ppermute(value, axis, [(s, (s + steps) % count) for s in range(count)])


def sent_back(value, steps):
    sections, count = lax.axis_size("section"), lax.axis_size("expert")
    pairs = [
        (s * count + e, (s - 1) % sections * count + (e + steps) % count)
        for s in range(sections)
        for e in range(count)
    ]
    return lax.ppermute(value, ("section", "expert"), pairs)


def offsets_of(reach):
    return list(range(-reach, reach + 1))


def hosts_of(d, reach):
    return tuple(range(0, COPIES, 2)) if abs(d) == reach else tuple(range(COPIES))


def blocks_of(d, reach):
    return tuple((d + reach + 2 * reach * k) % (2 * reach * COPIES) for k in hosts_of(d, reach))


def selectors(routes_ref, here, experts):
    reach = experts // (2 * COPIES)
    tokens = routes_ref.shape[1]
    ids = lax.broadcasted_iota(jnp.int32, (experts, tokens), 0)
    picks = [routes_ref[k : k + 1, :] for k in range(2)]
    named = [jnp.where(ids == p, 1.0, 0.0) for p in picks]
    earlier = lax.broadcasted_iota(jnp.int32, (tokens, tokens), 0) < lax.broadcasted_iota(
        jnp.int32, (tokens, tokens), 1
    )
    before = jnp.dot(
        (named[0] + named[1]).astype(BF16),
        jnp.where(earlier, 1.0, 0.0).astype(BF16),
        preferred_element_type=F32,
    )
    row = lax.broadcasted_iota(jnp.int32, (experts * SUB, tokens), 0)
    main, ninth = [], []
    for p, hit in zip(picks, named):
        slot = jnp.sum(before * hit, axis=0, keepdims=True).astype(jnp.int32)
        block = p - here + reach
        block = jnp.where(block < 0, block + experts, block)
        block = jnp.where(block >= experts, block - experts, block)
        main.append(jnp.where(row == jnp.where(slot < SUB, block * SUB + slot, -1), 1.0, 0.0))
        ninth.append(jnp.where((row >> 3) == jnp.where(slot == SUB, block, -1), 1.0, 0.0))
    return main, ninth, row & (SUB - 1)


def pack_kernel(here_ref, routes_ref, combine_ref, rows_ref, grads_ref, *outs, experts):
    reach = experts // (2 * COPIES)
    width = rows_ref.shape[1]
    fold = width // SUB
    main, ninth, sub = selectors(routes_ref, here_ref[0], experts)
    weights = [combine_ref[k : k + 1, :].astype(F32) for k in range(2)]
    for kind, ref in enumerate((rows_ref, grads_ref)):
        if kind == 0:
            pick = main[0] + main[1]
            pick9 = ninth[0] + ninth[1]
        else:
            pick = main[0] * weights[0] + main[1] * weights[1]
            pick9 = ninth[0] * weights[0] + ninth[1] * weights[1]
        body = jnp.dot(pick.astype(BF16), ref[...], preferred_element_type=F32)
        tail = jnp.zeros((experts * SUB, fold), F32)
        for s in range(SUB):
            tail = tail + jnp.dot(
                jnp.where(sub == s, pick9, 0.0).astype(BF16),
                ref[:, s * fold : (s + 1) * fold],
                preferred_element_type=F32,
            )
        for d, out in zip(offsets_of(reach), outs):
            for i, b in enumerate(blocks_of(d, reach)):
                at = slice(b * SUB, (b + 1) * SUB)
                out[2 * i + kind, :, 0:width] = body[at, :].astype(BF16)
                out[2 * i + kind, :, width : width + fold] = tail[at, :].astype(BF16)


def pack(here, routes_t, combine_t, rows, grads, experts):
    reach = experts // (2 * COPIES)
    width = rows.shape[1]
    vmem = pl.BlockSpec(memory_space=pltpu.VMEM)
    shapes = [
        jax.ShapeDtypeStruct((2 * len(blocks_of(d, reach)), SUB, width + width // SUB), BF16)
        for d in offsets_of(reach)
    ]
    return pl.pallas_call(
        lambda *refs: pack_kernel(*refs, experts=experts),
        out_shape=shapes,
        in_specs=[pl.BlockSpec(memory_space=pltpu.SMEM)] + [vmem] * 4,
        out_specs=[vmem] * len(shapes),
        name="pack",
        interpret=INTERPRET,
    )(here, routes_t, combine_t, rows, grads)


def gather_blocks(blocks, scratch, folded, width, picks):
    fold = width // SUB
    count = len(blocks)
    for b, block in enumerate(blocks):
        scratch[b * SUB : (b + 1) * SUB, :] = block[:, 0:width]
        folded[b * SUB : (b + 1) * SUB, :] = block[:, width : width + fold]
    whole = folded[0 : count * SUB, :]
    for s in range(SUB):
        nine = jnp.dot(picks[s], whole, preferred_element_type=F32).astype(BF16)
        scratch[count * SUB : count * SUB + nine.shape[0], s * fold : (s + 1) * fold] = nine


def expert_kernel(*refs, experts):
    reach = experts // (2 * COPIES)
    offsets = offsets_of(reach)
    core_ref, refs = refs[0], refs[1:]
    arrived = refs[: len(offsets)]
    own_w = refs[len(offsets) : len(offsets) + 3]
    side_w, far_w = refs[len(offsets) + 3 : len(offsets) + 5]
    at = len(offsets) + 5
    returned = refs[at : at + len(offsets)]
    at += len(offsets)
    far_keep, far_give, side_keep, side_give, own_keep, own_give = refs[at : at + 6]
    x_ref, g_ref, folded = refs[at + 6 :]
    width = own_w[0].shape[0]
    ff = own_w[0].shape[1]
    fold = width // SUB
    by_hidden = (((1,), (1,)), ((), ()))
    by_rows = (((0,), (0,)), ((), ()))
    for k in range(COPIES):
        here = [(d, hosts_of(d, reach).index(k)) for d in offsets if k in hosts_of(d, reach)]
        count = len(here)
        padded = -(-count // SUB) * SUB
        rows = count * SUB + padded
        r0 = lax.broadcasted_iota(jnp.int32, (padded, count * SUB), 0)
        r1 = lax.broadcasted_iota(jnp.int32, (padded, count * SUB), 1)
        picks = [jnp.where(r1 == r0 * SUB + s, 1.0, 0.0).astype(BF16) for s in range(SUB)]
        blocks = [arrived[d + reach].at[2 * i] for d, i in here]
        gather_blocks(blocks, x_ref, folded, width, picks)
        blocks = [arrived[d + reach].at[2 * i + 1] for d, i in here]
        gather_blocks(blocks, g_ref, folded, width, picks)
        if k == 0:
            gate_w, up_w, down_w = [w[...] for w in own_w]
        elif k == 2:
            gate_w, up_w, down_w = [far_w[:, :, 0, i].reshape(width, ff) for i in range(3)]
        else:
            gate_w, up_w, down_w = [side_w[:, :, k // 2, i].reshape(width, ff) for i in range(3)]
        x = x_ref[0:rows, :]
        g = g_ref[0:rows, :]
        gate = jnp.dot(x, gate_w, preferred_element_type=F32)
        upper = jnp.dot(x, up_w, preferred_element_type=F32)
        d_hidden = jnp.dot(g, down_w, preferred_element_type=F32)
        sigma = jax.nn.sigmoid(gate)
        active = gate * sigma
        hidden = (active * upper).astype(BF16)
        weighed = jnp.sum(hidden.astype(F32) * d_hidden, axis=1, keepdims=True)
        d_gate = (d_hidden * upper * (sigma * (1.0 + gate * (1.0 - sigma)))).astype(BF16)
        d_up = (d_hidden * active).astype(BF16)
        slot_grad = lax.dot_general(d_gate, gate_w, by_hidden, preferred_element_type=F32)
        slot_grad = slot_grad + lax.dot_general(d_up, up_w, by_hidden, preferred_element_type=F32)
        nine = slot_grad[count * SUB :, :].astype(BF16)
        q0 = lax.broadcasted_iota(jnp.int32, (count * SUB, padded), 0)
        q1 = lax.broadcasted_iota(jnp.int32, (count * SUB, padded), 1)
        tail = jnp.zeros((count * SUB, fold), F32)
        spread = []
        for s in range(SUB):
            put = jnp.where(q0 == q1 * SUB + s, 1.0, 0.0).astype(BF16)
            spread.append(put)
            tail = tail + jnp.dot(put, nine[:, s * fold : (s + 1) * fold], preferred_element_type=F32)
        nine_sum = jnp.broadcast_to(weighed[count * SUB :, :], (padded, EXTRA)).astype(BF16)
        nine_sum = jnp.dot(spread[0], nine_sum, preferred_element_type=F32)
        lane = lax.broadcasted_iota(jnp.int32, (count * SUB, EXTRA), 1)
        extra = jnp.where(lane == 0, weighed[0 : count * SUB, :], jnp.where(lane == 1, nine_sum, 0.0))
        for b, (d, i) in enumerate(here):
            out = returned[d + reach]
            span = slice(b * SUB, (b + 1) * SUB)
            out[i, :, 0:width] = slot_grad[span, :].astype(BF16)
            out[i, :, width : width + fold] = tail[span, :].astype(BF16)
            out[i, :, width + fold : width + fold + EXTRA] = extra[span, :].astype(BF16)
        for i, (left, right) in enumerate(((x, d_gate), (x, d_up), (g, hidden))):
            cols = slice(i * ff, (i + 1) * ff)
            term = lax.dot_general(left, right, by_rows, preferred_element_type=F32).astype(BF16)
            chips = far_keep.shape[0]
            term = term.reshape(chips, CORES, -1, ff)
            at = k // 2 if k % 2 else 0
            keep, give = ((own_keep, own_give), (side_keep, side_give), (far_keep, far_give))[
                1 if k % 2 else k
            ]
            for core in range(CORES):

                @pl.when(core_ref[0] == core)
                def _(term=term, core=core, keep=keep, give=give, at=at, cols=cols):
                    keep[:, at, :, cols] = term[:, core]
                    give[:, at, :, cols] = term[:, 1 - core]


def run_experts(core, arrived, own_w, side_w, far_w, experts):
    reach = experts // (2 * COPIES)
    width, ff = own_w[0].shape
    fold = width // SUB
    chips = far_w.shape[1]
    vmem = pl.BlockSpec(memory_space=pltpu.VMEM)
    shapes = [
        jax.ShapeDtypeStruct((len(blocks_of(d, reach)), SUB, width + fold + EXTRA), BF16)
        for d in offsets_of(reach)
    ] + [
        jax.ShapeDtypeStruct((chips, hosts, width // (CORES * chips), 3 * ff), BF16)
        for hosts in (1, 1, 2, 2, 1, 1)
    ]
    count = 2 * reach + 1
    rows = count * SUB + -(-count // SUB) * SUB
    outs = pl.pallas_call(
        lambda *refs: expert_kernel(*refs, experts=experts),
        out_shape=shapes,
        in_specs=[pl.BlockSpec(memory_space=pltpu.SMEM)] + [vmem] * (len(arrived) + 5),
        out_specs=[vmem] * len(shapes),
        scratch_shapes=[
            pltpu.VMEM((rows, width), BF16),
            pltpu.VMEM((rows, width), BF16),
            pltpu.VMEM((count * SUB, fold), BF16),
        ],
        name="experts",
        interpret=INTERPRET,
    )(core, *arrived, *own_w, side_w, far_w)
    return outs[:-6], outs[-6:]


def scalars_kernel(here_ref, routes_ref, combine_ref, *refs, experts):
    reach = experts // (2 * COPIES)
    offsets = offsets_of(reach)
    combine_out, extra = refs[len(offsets) :]
    for d, ref in zip(offsets, refs):
        for i, b in enumerate(blocks_of(d, reach)):
            extra[b * SUB : (b + 1) * SUB, :] = ref[i].astype(F32)
    main, ninth, sub = selectors(routes_ref, here_ref[0], experts)
    for k in range(2):
        value = main[k] * extra[:, 0:1] + jnp.where(sub == 0, ninth[k], 0.0) * extra[:, 1:2]
        value = jnp.sum(value, axis=0, keepdims=True)
        combine_out[k : k + 1, :] = value / combine_ref[k : k + 1, :]


def unpack_kernel(here_ref, routes_ref, *refs, experts):
    reach = experts // (2 * COPIES)
    offsets = offsets_of(reach)
    grad_out, body, tail = refs[len(offsets) :]
    width = body.shape[1]
    fold = tail.shape[1]
    for d, ref in zip(offsets, refs):
        for i, b in enumerate(blocks_of(d, reach)):
            span = slice(b * SUB, (b + 1) * SUB)
            body[span, :] = ref[i, :, 0:width]
            tail[span, :] = ref[i, :, width : width + fold]
    main, ninth, sub = selectors(routes_ref, here_ref[0], experts)
    pick = (main[0] + main[1]).T.astype(BF16)
    nine = ninth[0] + ninth[1]
    for s in range(SUB):
        cols = slice(s * fold, (s + 1) * fold)
        total = jnp.dot(pick, body[:, cols], preferred_element_type=F32)
        total = total + jnp.dot(
            jnp.where(sub == s, nine, 0.0).T.astype(BF16), tail[...], preferred_element_type=F32
        )
        grad_out[:, cols] = total.astype(BF16)


def unpack_scalars(here, routes_t, combine_t, arrived, width, experts):
    vmem = pl.BlockSpec(memory_space=pltpu.VMEM)
    at = (width + width // SUB) // EXTRA
    lanes = [pl.BlockSpec((a.shape[0], SUB, EXTRA), lambda i: (0, 0, at)) for a in arrived]
    return pl.pallas_call(
        lambda *refs: scalars_kernel(*refs, experts=experts),
        grid=(1,),
        out_shape=jax.ShapeDtypeStruct(routes_t.shape, F32),
        in_specs=[pl.BlockSpec(memory_space=pltpu.SMEM), vmem, vmem] + lanes,
        out_specs=vmem,
        scratch_shapes=[pltpu.VMEM((experts * SUB, EXTRA), F32)],
        name="scalars",
        interpret=INTERPRET,
    )(here, routes_t, combine_t, *arrived)


def unpack(here, routes_t, arrived, width, experts):
    vmem = pl.BlockSpec(memory_space=pltpu.VMEM)
    return pl.pallas_call(
        lambda *refs: unpack_kernel(*refs, experts=experts),
        out_shape=jax.ShapeDtypeStruct((routes_t.shape[1], width), BF16),
        in_specs=[pl.BlockSpec(memory_space=pltpu.SMEM)] + [vmem] * (1 + len(arrived)),
        out_specs=vmem,
        scratch_shapes=[
            pltpu.VMEM((experts * SUB, width), BF16),
            pltpu.VMEM((experts * SUB, width // SUB), BF16),
        ],
        name="unpack",
        interpret=INTERPRET,
    )(here, routes_t, *arrived)


def over_chips(x):
    count = lax.axis_size("dp")
    groups = [list(range(c, count, CORES)) for c in range(CORES)]
    return lax.all_to_all(
        x, "dp", split_axis=0, concat_axis=0, tiled=True, axis_index_groups=groups
    )


def other_core(x):
    return lax.ppermute(x, "dp", [(i, i ^ 1) for i in range(lax.axis_size("dp"))])


def per_device(tokens_in, upstream, routes, combine, gate_proj, up_proj, down_proj):
    experts = lax.axis_size("expert")
    replicas = lax.axis_size("dp")
    reach = experts // (2 * COPIES)
    period = 2 * reach
    width = tokens_in.shape[2]
    tokens = tokens_in.shape[1]
    assert 9 * tokens == 4 * experts * (SUB + 1)
    here = lax.axis_index("expert").astype(jnp.int32).reshape(1)
    routes_t = routes[0].T
    combine_t = combine[0].T
    own_w = [w[0, 0] for w in (gate_proj, up_proj, down_proj)]
    part = width // replicas
    chips = replicas // CORES
    lane = lax.axis_index("dp")
    core = (lane % CORES).astype(jnp.int32)
    start = (core * chips + lane // CORES) * part
    offsets = offsets_of(reach)

    def spread(x):
        same = over_chips(jnp.broadcast_to(x[None], (chips,) + x.shape))
        other = other_core(same)
        low = jnp.where(core == 0, same, other)
        high = jnp.where(core == 0, other, same)
        return jnp.stack([low, high])

    piece = jnp.stack([lax.dynamic_slice_in_dim(w, start, part, 0) for w in own_w])
    side1 = shifted(piece, "expert", -period)
    side3 = shifted(piece, "expert", period)
    low = shifted(side1[:, : part // 2], "expert", -period)
    high = shifted(side3[:, part // 2 :], "expert", period)
    side_w = spread(jnp.stack([side1, side3]))
    far_w = spread(jnp.concatenate([low, high], axis=1)[None])
    packed = pack(here, routes_t, combine_t, tokens_in[0], upstream[0], experts)
    behind = shifted(jnp.concatenate([routes_t.astype(F32), combine_t.astype(F32)]), "section", -1)
    arrived = list(packed)
    for i, d in enumerate(offsets):
        if d:
            arrived[i] = shifted(packed[i], "expert", d)
    done, terms = run_experts(
        core.reshape(1), arrived, own_w, side_w, far_w, experts
    )
    back = []
    for i, d in enumerate(offsets):
        back.append(sent_back(done[i], -d))

    def summed(keep, give):
        got = other_core(give)
        both = (keep.astype(F32) + got.astype(F32)).astype(BF16)
        return over_chips(both).astype(F32).sum(axis=0)

    far_sum = summed(*terms[0:2])[0].astype(BF16)
    side_sum = summed(*terms[2:4])
    own_sum = summed(*terms[4:6])[0]
    low = shifted(far_sum[: part // 2], "expert", period)
    high = shifted(far_sum[part // 2 :], "expert", -period)
    joined = jnp.concatenate([side_sum[0, : part // 2] + low.astype(F32), side_sum[0, part // 2 :]])
    side1 = shifted(joined.astype(BF16), "expert", period)
    joined = jnp.concatenate([side_sum[1, : part // 2], side_sum[1, part // 2 :] + high.astype(F32)])
    side3 = shifted(joined.astype(BF16), "expert", -period)
    weight_grad = (own_sum + side1.astype(F32) + side3.astype(F32)) * (1.0 / replicas)
    routes_b = behind[:2].astype(jnp.int32)
    combine_grad = unpack_scalars(here, routes_b, behind[2:], back, width, experts)
    combine_grad = shifted(combine_grad, "section", 1)
    prev_grad = unpack(here, routes_b, back, width, experts)
    return prev_grad[None], weight_grad[None, None], combine_grad.astype(BF16).T[None]


def solution(mesh):
    rows = P("section", ("dp", "expert"), None)
    weights = P("section", "expert", None, None)

    return jax.shard_map(
        per_device,
        mesh=mesh,
        in_specs=(rows, rows, rows, rows, weights, weights, weights),
        out_specs=(rows, P("section", "expert", "dp", None), rows),
        check_vma=False,
    )
```

```python
import jax
import jax.numpy as jnp
from jax import lax
from jax.experimental import pallas as pl
from jax.experimental.pallas import tpu as pltpu
from jax.sharding import PartitionSpec as P


INTERPRET = False
F32 = jnp.float32
BF16 = jnp.bfloat16
SUB = 8
EXTRA = 128


COPIES = 4
CORES = 2


def shifted(value, axis, steps):
    count = lax.axis_size(axis)
    return lax.ppermute(value, axis, [(s, (s + steps) % count) for s in range(count)])


def offsets_of(reach):
    return list(range(-reach, reach + 1))


def hosts_of(d, reach):
    return tuple(range(0, COPIES, 2)) if abs(d) == reach else tuple(range(COPIES))


def blocks_of(d, reach):
    return tuple((d + reach + 2 * reach * k) % (2 * reach * COPIES) for k in hosts_of(d, reach))


def selectors(routes_ref, here, experts):
    reach = experts // (2 * COPIES)
    tokens = routes_ref.shape[1]
    ids = lax.broadcasted_iota(jnp.int32, (experts, tokens), 0)
    picks = [routes_ref[k : k + 1, :] for k in range(2)]
    named = [jnp.where(ids == p, 1.0, 0.0) for p in picks]
    earlier = lax.broadcasted_iota(jnp.int32, (tokens, tokens), 0) < lax.broadcasted_iota(
        jnp.int32, (tokens, tokens), 1
    )
    before = jnp.dot(
        (named[0] + named[1]).astype(BF16),
        jnp.where(earlier, 1.0, 0.0).astype(BF16),
        preferred_element_type=F32,
    )
    row = lax.broadcasted_iota(jnp.int32, (experts * SUB, tokens), 0)
    main, ninth = [], []
    for p, hit in zip(picks, named):
        slot = jnp.sum(before * hit, axis=0, keepdims=True).astype(jnp.int32)
        block = p - here + reach
        block = jnp.where(block < 0, block + experts, block)
        block = jnp.where(block >= experts, block - experts, block)
        main.append(jnp.where(row == jnp.where(slot < SUB, block * SUB + slot, -1), 1.0, 0.0))
        ninth.append(jnp.where((row >> 3) == jnp.where(slot == SUB, block, -1), 1.0, 0.0))
    return main, ninth, row & (SUB - 1)


def pack_kernel(here_ref, routes_ref, combine_ref, rows_ref, grads_ref, *outs, experts):
    reach = experts // (2 * COPIES)
    width = rows_ref.shape[1]
    fold = width // SUB
    main, ninth, sub = selectors(routes_ref, here_ref[0], experts)
    weights = [combine_ref[k : k + 1, :].astype(F32) for k in range(2)]
    for kind, ref in enumerate((rows_ref, grads_ref)):
        if kind == 0:
            pick = main[0] + main[1]
            pick9 = ninth[0] + ninth[1]
        else:
            pick = main[0] * weights[0] + main[1] * weights[1]
            pick9 = ninth[0] * weights[0] + ninth[1] * weights[1]
        body = jnp.dot(pick.astype(BF16), ref[...], preferred_element_type=F32)
        tail = jnp.zeros((experts * SUB, fold), F32)
        for s in range(SUB):
            tail = tail + jnp.dot(
                jnp.where(sub == s, pick9, 0.0).astype(BF16),
                ref[:, s * fold : (s + 1) * fold],
                preferred_element_type=F32,
            )
        for d, out in zip(offsets_of(reach), outs):
            for i, b in enumerate(blocks_of(d, reach)):
                at = slice(b * SUB, (b + 1) * SUB)
                out[2 * i + kind, :, 0:width] = body[at, :].astype(BF16)
                out[2 * i + kind, :, width : width + fold] = tail[at, :].astype(BF16)


def pack(here, routes_t, combine_t, rows, grads, experts):
    reach = experts // (2 * COPIES)
    width = rows.shape[1]
    vmem = pl.BlockSpec(memory_space=pltpu.VMEM)
    shapes = [
        jax.ShapeDtypeStruct((2 * len(blocks_of(d, reach)), SUB, width + width // SUB), BF16)
        for d in offsets_of(reach)
    ]
    return pl.pallas_call(
        lambda *refs: pack_kernel(*refs, experts=experts),
        out_shape=shapes,
        in_specs=[pl.BlockSpec(memory_space=pltpu.SMEM)] + [vmem] * 4,
        out_specs=[vmem] * len(shapes),
        name="pack",
        interpret=INTERPRET,
    )(here, routes_t, combine_t, rows, grads)


def gather_blocks(blocks, scratch, folded, width, picks):
    fold = width // SUB
    count = len(blocks)
    for b, block in enumerate(blocks):
        scratch[b * SUB : (b + 1) * SUB, :] = block[:, 0:width]
        folded[b * SUB : (b + 1) * SUB, :] = block[:, width : width + fold]
    whole = folded[0 : count * SUB, :]
    for s in range(SUB):
        nine = jnp.dot(picks[s], whole, preferred_element_type=F32).astype(BF16)
        scratch[count * SUB : count * SUB + nine.shape[0], s * fold : (s + 1) * fold] = nine


def expert_kernel(*refs, experts):
    reach = experts // (2 * COPIES)
    offsets = offsets_of(reach)
    core_ref, refs = refs[0], refs[1:]
    arrived = refs[: len(offsets)]
    own_w = refs[len(offsets) : len(offsets) + 3]
    side_hbm, far_hbm = refs[len(offsets) + 3 : len(offsets) + 5]
    at = len(offsets) + 5
    returned = refs[at : at + len(offsets)]
    at += len(offsets)
    far_keep, far_give, side_keep, side_give, own_keep, own_give = refs[at : at + 6]
    x_ref, g_ref, folded, side_w, far_w, term_ref, in_sems, out_sems = refs[at + 6 :]
    far_in = pltpu.make_async_copy(far_hbm, far_w, in_sems.at[0])
    side_in = pltpu.make_async_copy(side_hbm, side_w, in_sems.at[1])
    far_in.start()
    side_in.start()
    core = core_ref[0]
    flights = []
    width = own_w[0].shape[0]
    ff = own_w[0].shape[1]
    fold = width // SUB
    by_hidden = (((1,), (1,)), ((), ()))
    by_rows = (((0,), (0,)), ((), ()))
    for k in (0, 2, 1, 3):
        here = [(d, hosts_of(d, reach).index(k)) for d in offsets if k in hosts_of(d, reach)]
        count = len(here)
        padded = -(-count // SUB) * SUB
        rows = count * SUB + padded
        r0 = lax.broadcasted_iota(jnp.int32, (padded, count * SUB), 0)
        r1 = lax.broadcasted_iota(jnp.int32, (padded, count * SUB), 1)
        picks = [jnp.where(r1 == r0 * SUB + s, 1.0, 0.0).astype(BF16) for s in range(SUB)]
        blocks = [arrived[d + reach].at[2 * i] for d, i in here]
        gather_blocks(blocks, x_ref, folded, width, picks)
        blocks = [arrived[d + reach].at[2 * i + 1] for d, i in here]
        gather_blocks(blocks, g_ref, folded, width, picks)
        if k == 0:
            gate_w, up_w, down_w = [w[...] for w in own_w]
        elif k == 2:
            far_in.wait()
            gate_w, up_w, down_w = [far_w[:, :, 0, i].reshape(width, ff) for i in range(3)]
        else:
            if k == 1:
                side_in.wait()
            gate_w, up_w, down_w = [side_w[:, :, k // 2, i].reshape(width, ff) for i in range(3)]
        x = x_ref[0:rows, :]
        g = g_ref[0:rows, :]
        gate = jnp.dot(x, gate_w, preferred_element_type=F32)
        upper = jnp.dot(x, up_w, preferred_element_type=F32)
        d_hidden = jnp.dot(g, down_w, preferred_element_type=F32)
        sigma = jax.nn.sigmoid(gate)
        active = gate * sigma
        hidden = (active * upper).astype(BF16)
        weighed = jnp.sum(hidden.astype(F32) * d_hidden, axis=1, keepdims=True)
        d_gate = (d_hidden * upper * (sigma * (1.0 + gate * (1.0 - sigma)))).astype(BF16)
        d_up = (d_hidden * active).astype(BF16)
        slot_grad = lax.dot_general(d_gate, gate_w, by_hidden, preferred_element_type=F32)
        slot_grad = slot_grad + lax.dot_general(d_up, up_w, by_hidden, preferred_element_type=F32)
        nine = slot_grad[count * SUB :, :].astype(BF16)
        q0 = lax.broadcasted_iota(jnp.int32, (count * SUB, padded), 0)
        q1 = lax.broadcasted_iota(jnp.int32, (count * SUB, padded), 1)
        tail = jnp.zeros((count * SUB, fold), F32)
        spread = []
        for s in range(SUB):
            put = jnp.where(q0 == q1 * SUB + s, 1.0, 0.0).astype(BF16)
            spread.append(put)
            tail = tail + jnp.dot(put, nine[:, s * fold : (s + 1) * fold], preferred_element_type=F32)
        nine_sum = jnp.broadcast_to(weighed[count * SUB :, :], (padded, EXTRA)).astype(BF16)
        nine_sum = jnp.dot(spread[0], nine_sum, preferred_element_type=F32)
        lane = lax.broadcasted_iota(jnp.int32, (count * SUB, EXTRA), 1)
        extra = jnp.where(lane == 0, weighed[0 : count * SUB, :], jnp.where(lane == 1, nine_sum, 0.0))
        for b, (d, i) in enumerate(here):
            out = returned[d + reach]
            span = slice(b * SUB, (b + 1) * SUB)
            out[i, :, 0:width] = slot_grad[span, :].astype(BF16)
            out[i, :, width : width + fold] = tail[span, :].astype(BF16)
            out[i, :, width + fold : width + fold + EXTRA] = extra[span, :].astype(BF16)
        for i, (left, right) in enumerate(((x, d_gate), (x, d_up), (g, hidden))):
            cols = slice(i * ff, (i + 1) * ff)
            term = lax.dot_general(left, right, by_rows, preferred_element_type=F32).astype(BF16)
            term_ref[k, :, :, :, cols] = term.reshape(term_ref.shape[1:4] + (ff,))
        keep, give = ((own_keep, own_give), (side_keep, side_give), (far_keep, far_give))[
            1 if k % 2 else k
        ]
        to = k // 2 if k % 2 else 0
        flights += [
            pltpu.make_async_copy(term_ref.at[k, :, core], keep.at[:, to], out_sems.at[k, 0]),
            pltpu.make_async_copy(term_ref.at[k, :, 1 - core], give.at[:, to], out_sems.at[k, 1]),
        ]
        for flight in flights[-2:]:
            flight.start()
    for flight in flights:
        flight.wait()


def run_experts(core, arrived, own_w, side_w, far_w, experts):
    reach = experts // (2 * COPIES)
    width, ff = own_w[0].shape
    fold = width // SUB
    chips = far_w.shape[1]
    vmem = pl.BlockSpec(memory_space=pltpu.VMEM)
    anywhere = pl.BlockSpec(memory_space=pl.ANY)
    shapes = [
        jax.ShapeDtypeStruct((len(blocks_of(d, reach)), SUB, width + fold + EXTRA), BF16)
        for d in offsets_of(reach)
    ] + [
        jax.ShapeDtypeStruct((chips, hosts, width // (CORES * chips), 3 * ff), BF16)
        for hosts in (1, 1, 2, 2, 1, 1)
    ]
    count = 2 * reach + 1
    rows = count * SUB + -(-count // SUB) * SUB
    outs = pl.pallas_call(
        lambda *refs: expert_kernel(*refs, experts=experts),
        out_shape=shapes,
        in_specs=[pl.BlockSpec(memory_space=pltpu.SMEM)]
        + [vmem] * (len(arrived) + 3)
        + [anywhere] * 2,
        out_specs=[vmem] * len(arrived) + [anywhere] * 6,
        scratch_shapes=[
            pltpu.VMEM((rows, width), BF16),
            pltpu.VMEM((rows, width), BF16),
            pltpu.VMEM((count * SUB, fold), BF16),
            pltpu.VMEM(side_w.shape, BF16),
            pltpu.VMEM(far_w.shape, BF16),
            pltpu.VMEM((COPIES, chips, CORES, width // (CORES * chips), 3 * ff), BF16),
            pltpu.SemaphoreType.DMA((2,)),
            pltpu.SemaphoreType.DMA((COPIES, 2)),
        ],
        name="experts",
        interpret=INTERPRET,
    )(core, *arrived, *own_w, side_w, far_w)
    return outs[:-6], outs[-6:]


def unpack_kernel(here_ref, routes_ref, combine_ref, *refs, experts):
    reach = experts // (2 * COPIES)
    offsets = offsets_of(reach)
    grad_out, combine_out, body, tail, extra = refs[len(offsets) :]
    width = body.shape[1]
    fold = tail.shape[1]
    for d, ref in zip(offsets, refs):
        for i, b in enumerate(blocks_of(d, reach)):
            span = slice(b * SUB, (b + 1) * SUB)
            body[span, :] = ref[i, :, 0:width]
            tail[span, :] = ref[i, :, width : width + fold]
            extra[span, :] = ref[i, :, width + fold : width + fold + EXTRA].astype(F32)
    main, ninth, sub = selectors(routes_ref, here_ref[0], experts)
    pick = (main[0] + main[1]).T.astype(BF16)
    nine = ninth[0] + ninth[1]
    for s in range(SUB):
        cols = slice(s * fold, (s + 1) * fold)
        total = jnp.dot(pick, body[:, cols], preferred_element_type=F32)
        total = total + jnp.dot(
            jnp.where(sub == s, nine, 0.0).T.astype(BF16), tail[...], preferred_element_type=F32
        )
        grad_out[:, cols] = total.astype(BF16)
    for k in range(2):
        value = main[k] * extra[:, 0:1] + jnp.where(sub == 0, ninth[k], 0.0) * extra[:, 1:2]
        value = jnp.sum(value, axis=0, keepdims=True)
        combine_out[k : k + 1, :] = value / combine_ref[k : k + 1, :].astype(F32)


def unpack(here, routes_t, combine_t, arrived, width, experts):
    tokens = routes_t.shape[1]
    vmem = pl.BlockSpec(memory_space=pltpu.VMEM)
    return pl.pallas_call(
        lambda *refs: unpack_kernel(*refs, experts=experts),
        out_shape=[
            jax.ShapeDtypeStruct((tokens, width), BF16),
            jax.ShapeDtypeStruct((2, tokens), F32),
        ],
        in_specs=[pl.BlockSpec(memory_space=pltpu.SMEM)] + [vmem] * (2 + len(arrived)),
        out_specs=[vmem] * 2,
        scratch_shapes=[
            pltpu.VMEM((experts * SUB, width), BF16),
            pltpu.VMEM((experts * SUB, width // SUB), BF16),
            pltpu.VMEM((experts * SUB, EXTRA), F32),
        ],
        name="unpack",
        interpret=INTERPRET,
    )(here, routes_t, combine_t, *arrived)


def over_chips(x):
    count = lax.axis_size("dp")
    groups = [list(range(c, count, CORES)) for c in range(CORES)]
    return lax.all_to_all(
        x, "dp", split_axis=0, concat_axis=0, tiled=True, axis_index_groups=groups
    )


def other_core(x):
    return lax.ppermute(x, "dp", [(i, i ^ 1) for i in range(lax.axis_size("dp"))])


def per_device(tokens_in, upstream, routes, combine, gate_proj, up_proj, down_proj):
    experts = lax.axis_size("expert")
    replicas = lax.axis_size("dp")
    reach = experts // (2 * COPIES)
    period = 2 * reach
    width = tokens_in.shape[2]
    tokens = tokens_in.shape[1]
    assert 9 * tokens == 4 * experts * (SUB + 1)
    here = lax.axis_index("expert").astype(jnp.int32).reshape(1)
    routes_t = routes[0].T
    combine_t = combine[0].T
    own_w = [w[0, 0] for w in (gate_proj, up_proj, down_proj)]
    part = width // replicas
    chips = replicas // CORES
    lane = lax.axis_index("dp")
    core = (lane % CORES).astype(jnp.int32)
    start = (core * chips + lane // CORES) * part
    offsets = offsets_of(reach)

    def spread(x):
        same = over_chips(jnp.broadcast_to(x[None], (chips,) + x.shape))
        other = other_core(same)
        low = jnp.where(core == 0, same, other)
        high = jnp.where(core == 0, other, same)
        return jnp.stack([low, high])

    piece = jnp.stack([lax.dynamic_slice_in_dim(w, start, part, 0) for w in own_w])
    side1 = shifted(piece, "expert", -period)
    side3 = shifted(piece, "expert", period)
    low = shifted(side1[:, : part // 2], "expert", -period)
    high = shifted(side3[:, part // 2 :], "expert", period)
    side_w = spread(jnp.stack([side1, side3]))
    far_w = spread(jnp.concatenate([low, high], axis=1)[None])
    packed = pack(here, routes_t, combine_t, tokens_in[0], upstream[0], experts)
    arrived = list(packed)
    for i, d in enumerate(offsets):
        if d:
            arrived[i] = shifted(packed[i], "expert", d)
    done, terms = run_experts(
        core.reshape(1), arrived, own_w, side_w, far_w, experts
    )
    back = list(done)
    for i, d in enumerate(offsets):
        if d:
            back[i] = shifted(done[i], "expert", -d)

    def summed(keep, give):
        got = other_core(give)
        both = (keep.astype(F32) + got.astype(F32)).astype(BF16)
        return over_chips(both).astype(F32).sum(axis=0)

    far_sum = summed(*terms[0:2])[0].astype(BF16)
    side_sum = summed(*terms[2:4])
    own_sum = summed(*terms[4:6])[0]
    low = shifted(far_sum[: part // 2], "expert", period)
    high = shifted(far_sum[part // 2 :], "expert", -period)
    joined = jnp.concatenate([side_sum[0, : part // 2] + low.astype(F32), side_sum[0, part // 2 :]])
    side1 = shifted(joined.astype(BF16), "expert", period)
    joined = jnp.concatenate([side_sum[1, : part // 2], side_sum[1, part // 2 :] + high.astype(F32)])
    side3 = shifted(joined.astype(BF16), "expert", -period)
    weight_grad = (own_sum + side1.astype(F32) + side3.astype(F32)) * (1.0 / replicas)
    token_grad, combine_grad = unpack(here, routes_t, combine_t, back, width, experts)
    prev_grad = shifted(token_grad[None], "section", -1)
    return prev_grad, weight_grad[None, None], combine_grad.astype(BF16).T[None]


def solution(mesh):
    rows = P("section", ("dp", "expert"), None)
    weights = P("section", "expert", None, None)

    return jax.shard_map(
        per_device,
        mesh=mesh,
        in_specs=(rows, rows, rows, rows, weights, weights, weights),
        out_specs=(rows, P("section", "expert", "dp", None), rows),
        check_vma=False,
    )
```
